32 devices in a mesh: dp: 8 (over y, x, core), tensor: 4 (over z).
Axes of the slice: x: 2, y: 2, z: 4, core: 2. Of those that a mesh axis runs over, the one named last changes fastest.
Arguments:
- block_input: float32 [8, 736, 1152], P('dp', 'tensor'), may hold values from -6 to 6
- key_valid: int32 [8, 736], P('dp'), may hold values from 0 to 1, as said below
- mixgain: bfloat16 [2, 1152], P(None, 'dp'), may hold values from 0.5 to 1.5
- mixbias: bfloat16 [2, 1152], P(None, 'dp'), may hold values from -3 to 3
- inproj_weight: bfloat16 [2, 3, 1152, 1152], P(None, None, 'dp', 'tensor'), may hold values from -1 to 1
- querybias: bfloat16 [2, 1152], P(None, 'tensor'), may hold values from -3 to 3
- valuebias: bfloat16 [2, 1152], P(None, 'tensor'), may hold values from -3 to 3
- outproj_weight: bfloat16 [2, 1152, 1152], P(None, 'tensor', 'dp'), may hold values from -3 to 3
- outbias: bfloat16 [2, 1152], P(None, 'dp'), may hold values from -3 to 3
- ffgain: bfloat16 [2, 1152], P(None, 'dp'), may hold values from 0.5 to 1.5
- ffbias: bfloat16 [2, 1152], P(None, 'dp'), may hold values from -3 to 3
- expand_weight: bfloat16 [2, 1152, 4304], P(None, 'dp', 'tensor'), may hold values from -0.1875 to 0.1875
- expbias: bfloat16 [2, 4304], P(None, 'tensor'), may hold values from -3 to 3
- contract_weight: bfloat16 [2, 4304, 1152], P(None, 'tensor', 'dp'), may hold values from -0.25 to 0.25
- conbias: bfloat16 [2, 1152], P(None, 'dp'), may hold values from -4 to 4
- cotangent: float32 [8, 736, 1152], P('dp', 'tensor'), may hold values from -6 to 6
Outputs:
- block_output: float32 [8, 736, 1152], P('dp', 'tensor')
- input_gradient: float32 [8, 736, 1152], P('dp', 'tensor')
- mixgain_gradient: float32 [2, 1152], P(None, 'dp')
- mixbias_gradient: float32 [2, 1152], P(None, 'dp')
- inproj_gradient: float32 [2, 3, 1152, 1152], P(None, None, 'dp', 'tensor')
- querybias_gradient: float32 [2, 1152], P(None, 'tensor')
- valuebias_gradient: float32 [2, 1152], P(None, 'tensor')
- outproj_gradient: float32 [2, 1152, 1152], P(None, 'tensor', 'dp')
- outbias_gradient: float32 [2, 1152], P(None, 'dp')
- ffgain_gradient: float32 [2, 1152], P(None, 'dp')
- ffbias_gradient: float32 [2, 1152], P(None, 'dp')
- expand_gradient: float32 [2, 1152, 4304], P(None, 'dp', 'tensor')
- expbias_gradient: float32 [2, 4304], P(None, 'tensor')
- contract_gradient: float32 [2, 4304, 1152], P(None, 'tensor', 'dp')
- conbias_gradient: float32 [2, 1152], P(None, 'dp')
The draws below stay inside these ranges and needn't reach their ends.
Inputs may be any that keep to these rules, and one draw needn't show every extreme that they name: `key_valid`: each image's row is 1 on a first run of positions and 0 after it; every image has from 552 to 736 ones, and both ends occur in every draw.
All inputs are finite; a program needn't handle non-finite values.
Results may differ from the reference program's by a relative error of at most 0.033.
Values may be sent and summed in bfloat16 or wider, within the bound.
A program may use at most 192 MiB of HBM per device.

```python
import jax
import jax.numpy as jnp
from jax import lax

HEADS = 16
HEAD_DIM = 72
D = 1152
FF = 4304
SEQ = 736
LAYERS = 2
IMAGES = 8
N_TENSOR = 4


def draw_key_valid(key, part):
    length_key, order_key = jax.random.split(key)
    shortest = SEQ - SEQ // 4
    lengths = jax.random.randint(length_key, (IMAGES,), shortest, SEQ + 1)
    ordering = jax.random.permutation(order_key, IMAGES)
    lengths = lengths.at[ordering[0]].set(SEQ).at[ordering[1]].set(shortest)
    positions = jnp.arange(SEQ, dtype=jnp.int32)
    return (positions[None, :] < lengths[:, None]).astype(jnp.int32)


def draw_inproj_weight(key, part):
    noise_key = jax.random.fold_in(key, 0)
    base = jax.random.truncated_normal(noise_key, -4.0, 4.0, (LAYERS, 3, D, D), jnp.float32) * float(D) ** (-0.5)
    return base.astype(jnp.bfloat16)


def strengthened(drawn, own_key, source, target, shards_of, factor):
    def block_of(axis_at):
        return (jnp.arange(drawn.shape[axis_at]) // (drawn.shape[axis_at] // shards_of)).reshape((-1,) + (1,) * (drawn.ndim - 1 - axis_at))

    one_side = jax.random.permutation(own_key, shards_of)[block_of(target)]
    other_side = (block_of(target) + shards_of // 2) % shards_of
    return jnp.where((block_of(source) == one_side) | (block_of(source) == other_side), factor * drawn, drawn)


def level_of(stream_key, dims, cuts, least, largest):
    gain = 1.0
    for dim, shards_of in cuts:
        draws = jax.random.uniform(jax.random.fold_in(jax.random.fold_in(stream_key, 6), dim), (shards_of,), jnp.float32, least / len(cuts), largest / len(cuts))
        gain = gain * jnp.repeat(jnp.exp(draws), dims[dim] // shards_of).reshape((-1,) + (1,) * (len(dims) - 1 - dim))
    return gain


def centred(own_key, extent, scale, most, cuts=(), held_as=jnp.bfloat16):
    array = scale * jax.random.normal(own_key, extent, jnp.float32)
    if cuts:
        array = array * level_of(own_key, extent, cuts, -0.22, 0.18)
    return jnp.clip(array, -most, most).astype(held_as)


def bell_draw_with(stream_key, extent, scale, bound, pieces, heavy, kind=jnp.bfloat16):
    drawn = scale * jax.random.normal(stream_key, extent, jnp.float32)
    if pieces:
        drawn = drawn * level_of(stream_key, extent, pieces, -0.22, 0.18)
    return jnp.clip(strengthened(drawn, jax.random.fold_in(stream_key, 3), *heavy), -bound, bound).astype(kind)


def setup_inputs(seed: int = 0) -> dict:
    keys = jax.random.split(jax.random.key(seed), 17)
    block_input = centred(keys[0], (IMAGES, SEQ, D), 1.0, 6.0, ((0, 8), (1, 4)), jnp.float32)
    key_valid = draw_key_valid(jax.random.fold_in(keys[16], 71), 0)
    mixgain = jnp.clip(1.0 + 0.1 * jax.random.normal(keys[2], (LAYERS, D), jnp.float32), 0.5, 1.5).astype(jnp.bfloat16)
    mixbias = centred(keys[3], (LAYERS, D), 0.5, 3.0, ((1, 8),))
    inproj_weight = draw_inproj_weight(jax.random.fold_in(keys[16], 71), 0)
    querybias = centred(keys[5], (LAYERS, D), 0.5, 3.0, ((1, 4),))
    valuebias = centred(keys[6], (LAYERS, D), 0.5, 3.0, ((1, 4),))
    outproj_weight = centred(keys[7], (LAYERS, D, D), (max(D // 256, 1)) ** -0.5, 3.0, ((1, 4), (2, 8)))
    outbias = centred(keys[8], (LAYERS, D), 0.5, 3.0, ((1, 8),))
    ffgain = jnp.clip(1.0 + 0.1 * jax.random.normal(keys[9], (LAYERS, D), jnp.float32), 0.5, 1.5).astype(jnp.bfloat16)
    ffbias = centred(keys[10], (LAYERS, D), 0.5, 3.0, ((1, 8),))
    expand_weight = centred(keys[11], (LAYERS, D, FF), D ** -0.5, 0.1875, ((1, 8), (2, 4)))
    expbias = centred(keys[12], (LAYERS, FF), 0.5, 3.0, ((1, 4),))
    contract_weight = centred(keys[13], (LAYERS, FF, D), (max(FF // 8, 1)) ** -0.5, 0.25, ((1, 4), (2, 8)))
    conbias = centred(keys[14], (LAYERS, D), 1.0, 4.0, ((1, 8),))
    cotangent = bell_draw_with(keys[15], (IMAGES, SEQ, D), 1.0, 6.0, ((0, 8), (1, 4)), (0, 2, 8, 2.0), jnp.float32)
    return dict(block_input=block_input, key_valid=key_valid, mixgain=mixgain, mixbias=mixbias, inproj_weight=inproj_weight, querybias=querybias, valuebias=valuebias, outproj_weight=outproj_weight, outbias=outbias, ffgain=ffgain, ffbias=ffbias, expand_weight=expand_weight, expbias=expbias, contract_weight=contract_weight, conbias=conbias, cotangent=cotangent)


norm_epsilon = 1e-06
gelu_scale = 0.7978845608028654
gelu_cubic = 0.044715
masked_score = -1e+30

def layer_norm(matrix_rows, norm_gain, norm_shift):
    centered = matrix_rows - lax.optimization_barrier(jnp.mean(matrix_rows, axis=-1, keepdims=True))
    inverse = lax.rsqrt(lax.optimization_barrier(jnp.mean(centered * centered, axis=-1, keepdims=True)) + norm_epsilon)
    normed = centered * inverse
    return (normed * norm_gain.astype(jnp.float32) + norm_shift.astype(jnp.float32), normed, inverse)

def norm_backward(upstream, normed, inverse, norm_gain):
    scaled = upstream * norm_gain.astype(jnp.float32)
    mean_first = lax.optimization_barrier(jnp.mean(scaled, axis=-1, keepdims=True))
    mean_second = lax.optimization_barrier(jnp.mean(scaled * normed, axis=-1, keepdims=True))
    return inverse * (scaled - mean_first - normed * mean_second)

def gelu_parts(preact):
    tanh_part = jnp.tanh(gelu_scale * (preact + gelu_cubic * preact * preact * preact))
    gelu_value = 0.5 * preact * (1.0 + tanh_part)
    gelu_slope = 0.5 * (1.0 + tanh_part) + 0.5 * preact * (1.0 - tanh_part * tanh_part) * gelu_scale * (1.0 + 3.0 * gelu_cubic * preact * preact)
    return (gelu_value, gelu_slope)

def masked_scores(queries, keys_half, usable, factor):
    scores = jnp.einsum('qhd,khd->hqk', queries.astype(jnp.float32), keys_half.astype(jnp.float32)) * factor
    return jnp.where(usable[None, None, :], scores, masked_score)

def attend(queries, keys_half, values_half, usable, factor):
    scores = masked_scores(queries, keys_half, usable, factor)
    highest = lax.optimization_barrier(jnp.max(scores, axis=-1, keepdims=True))
    log_total = highest + jnp.log(lax.optimization_barrier(jnp.sum(jnp.exp(scores - highest), axis=-1, keepdims=True)))
    weights = jnp.exp(scores - log_total).astype(jnp.bfloat16)
    mixed_out = jnp.einsum('hqk,khd->qhd', weights.astype(jnp.float32), values_half.astype(jnp.float32))
    return (mixed_out.astype(jnp.bfloat16), log_total)

def attend_backward(queries, keys_half, values_half, usable, log_total, upstream, factor):
    weights = jnp.exp(masked_scores(queries, keys_half, usable, factor) - log_total)
    weights_half = weights.astype(jnp.bfloat16)
    upstream_wide = upstream.astype(jnp.float32)
    value_grad = jnp.einsum('hqk,qhd->khd', weights_half.astype(jnp.float32), upstream_wide)
    weight_grad = jnp.einsum('qhd,khd->hqk', upstream_wide, values_half.astype(jnp.float32))
    inner_sum = lax.optimization_barrier(jnp.sum(weights * weight_grad, axis=-1, keepdims=True))
    score_grad = (weights * (weight_grad - inner_sum) * factor).astype(jnp.bfloat16).astype(jnp.float32)
    query_grad = jnp.einsum('hqk,khd->qhd', score_grad, keys_half.astype(jnp.float32))
    key_grad = jnp.einsum('hqk,qhd->khd', score_grad, queries.astype(jnp.float32))
    return (query_grad, key_grad, value_grad)

def rounded_total(terms):
    rounded = lax.optimization_barrier(terms.astype(jnp.bfloat16))
    return lax.optimization_barrier(jnp.sum(rounded.astype(jnp.float32), axis=0))

def split_product(left_half, right_half):
    row_count = left_half.shape[0]
    out_width = right_half.shape[1]
    terms = jnp.einsum('stk,tkd->tsd', left_half.reshape(row_count, N_TENSOR, -1).astype(jnp.float32), right_half.reshape(N_TENSOR, -1, out_width).astype(jnp.float32))
    return rounded_total(terms)

def reference(block_input, key_valid, mixgain, mixbias, inproj_weight, querybias, valuebias, outproj_weight, outbias, ffgain, ffbias, expand_weight, expbias, contract_weight, conbias, cotangent):
    factor = float(HEAD_DIM) ** (-0.5)
    head_shape = (SEQ, HEADS, HEAD_DIM)

    def one_image(totals, inputs):
        image_rows, valid_row, image_cotangent = inputs
        usable = valid_row > 0
        residual = image_rows
        stored = []
        for layer_index in range(LAYERS):
            mix_value, mix_normed, mix_inverse = layer_norm(residual, mixgain[layer_index], mixbias[layer_index])
            mix_half = mix_value.astype(jnp.bfloat16)
            queries = (jnp.dot(mix_half, inproj_weight[layer_index, 0], preferred_element_type=jnp.float32) + querybias[layer_index].astype(jnp.float32)).astype(jnp.bfloat16).reshape(head_shape)
            keys_half = jnp.dot(mix_half, inproj_weight[layer_index, 1], preferred_element_type=jnp.float32).astype(jnp.bfloat16).reshape(head_shape)
            values_half = (jnp.dot(mix_half, inproj_weight[layer_index, 2], preferred_element_type=jnp.float32) + valuebias[layer_index].astype(jnp.float32)).astype(jnp.bfloat16).reshape(head_shape)
            heads_out, log_total = attend(queries, keys_half, values_half, usable, factor)
            heads_flat = heads_out.reshape(SEQ, D)
            middle = residual + split_product(heads_flat, outproj_weight[layer_index]) + outbias[layer_index].astype(jnp.float32)
            ff_value, ff_normed, ff_inverse = layer_norm(middle, ffgain[layer_index], ffbias[layer_index])
            ff_half = ff_value.astype(jnp.bfloat16)
            preact = jnp.dot(ff_half, expand_weight[layer_index], preferred_element_type=jnp.float32) + expbias[layer_index].astype(jnp.float32)
            gelu_value, gelu_slope = gelu_parts(preact)
            hidden_half = gelu_value.astype(jnp.bfloat16)
            stored.append((mix_normed, mix_inverse, mix_half, queries, keys_half, values_half, log_total, heads_flat, ff_normed, ff_inverse, ff_half, gelu_slope, hidden_half))
            residual = middle + split_product(hidden_half, contract_weight[layer_index]) + conbias[layer_index].astype(jnp.float32)
        output_rows = residual
        upstream = image_cotangent
        totals = list(totals)
        for layer_index in reversed(range(LAYERS)):
            mix_normed, mix_inverse, mix_half, queries, keys_half, values_half, log_total, heads_flat, ff_normed, ff_inverse, ff_half, gelu_slope, hidden_half = stored[layer_index]
            upstream_half = upstream.astype(jnp.bfloat16)
            contract_grad = jnp.dot(hidden_half.T, upstream_half, preferred_element_type=jnp.float32)
            preact_grad = jnp.dot(upstream_half, contract_weight[layer_index].T, preferred_element_type=jnp.float32) * gelu_slope
            preact_half = preact_grad.astype(jnp.bfloat16)
            expand_grad = jnp.dot(ff_half.T, preact_half, preferred_element_type=jnp.float32)
            ff_back = split_product(preact_half, expand_weight[layer_index].T)
            middle_grad = upstream + norm_backward(ff_back, ff_normed, ff_inverse, ffgain[layer_index])
            middle_half = middle_grad.astype(jnp.bfloat16)
            outproj_grad = jnp.dot(heads_flat.T, middle_half, preferred_element_type=jnp.float32)
            heads_grad = jnp.dot(middle_half, outproj_weight[layer_index].T, preferred_element_type=jnp.float32).astype(jnp.bfloat16).reshape(head_shape)
            query_grad, key_grad, value_grad = attend_backward(queries, keys_half, values_half, usable, log_total, heads_grad, factor)
            proj_grad = jnp.stack([query_grad, key_grad, value_grad]).reshape(3, SEQ, D)
            proj_half = proj_grad.astype(jnp.bfloat16)
            inproj_grad = jnp.einsum('sd,cse->cde', mix_half.astype(jnp.float32), proj_half.astype(jnp.float32))
            weight_turned = jnp.transpose(inproj_weight[layer_index], (0, 2, 1)).reshape(3, N_TENSOR, -1, D)
            terms = jnp.einsum('cstk,ctkd->tsd', proj_half.reshape(3, SEQ, N_TENSOR, -1).astype(jnp.float32), weight_turned.astype(jnp.float32))
            mix_back = rounded_total(terms)
            upstream_next = middle_grad + norm_backward(mix_back, mix_normed, mix_inverse, mixgain[layer_index])
            updates = (lax.optimization_barrier(jnp.sum(mix_back * mix_normed, axis=0)), lax.optimization_barrier(jnp.sum(mix_back, axis=0)), inproj_grad, lax.optimization_barrier(jnp.sum(proj_grad[0], axis=0)), lax.optimization_barrier(jnp.sum(proj_grad[2], axis=0)), outproj_grad, lax.optimization_barrier(jnp.sum(middle_grad, axis=0)), lax.optimization_barrier(jnp.sum(ff_back * ff_normed, axis=0)), lax.optimization_barrier(jnp.sum(ff_back, axis=0)), expand_grad, lax.optimization_barrier(jnp.sum(preact_grad, axis=0)), contract_grad, lax.optimization_barrier(jnp.sum(upstream, axis=0)))
            totals = [running.at[layer_index].add(update) for running, update in zip(totals, updates)]
            upstream = upstream_next
        return (tuple(totals), (output_rows, upstream))
    starting = (jnp.zeros((LAYERS, D), jnp.float32), jnp.zeros((LAYERS, D), jnp.float32), jnp.zeros((LAYERS, 3, D, D), jnp.float32), jnp.zeros((LAYERS, D), jnp.float32), jnp.zeros((LAYERS, D), jnp.float32), jnp.zeros((LAYERS, D, D), jnp.float32), jnp.zeros((LAYERS, D), jnp.float32), jnp.zeros((LAYERS, D), jnp.float32), jnp.zeros((LAYERS, D), jnp.float32), jnp.zeros((LAYERS, D, FF), jnp.float32), jnp.zeros((LAYERS, FF), jnp.float32), jnp.zeros((LAYERS, FF, D), jnp.float32), jnp.zeros((LAYERS, D), jnp.float32))
    totals, outputs = lax.scan(one_image, starting, (block_input, key_valid, cotangent))
    block_output, input_gradient = outputs
    return (block_output, input_gradient, totals[0], totals[1], totals[2], totals[3], totals[4], totals[5], totals[6], totals[7], totals[8], totals[9], totals[10], totals[11], totals[12])
```

```python
import functools

import jax
import jax.numpy as jnp
from jax import lax
from jax.experimental import pallas as pl
from jax.experimental.pallas import tpu as pltpu
from jax.sharding import PartitionSpec as P


MESH = pl.DeviceIdType.MESH

HEAD_DIM = 72


norm_epsilon = 1e-06
gelu_scale = 0.7978845608028654
gelu_cubic = 0.044715
masked_score = -1e30


def layer_norm(matrix_rows, norm_gain, norm_shift):
    centered = matrix_rows - jnp.mean(matrix_rows, axis=-1, keepdims=True)
    inverse = lax.rsqrt(jnp.mean(centered * centered, axis=-1, keepdims=True) + norm_epsilon)
    normed = centered * inverse
    return (
        normed * norm_gain.astype(jnp.float32) + norm_shift.astype(jnp.float32),
        normed,
        inverse,
    )


def norm_backward(upstream, normed, inverse, norm_gain):
    scaled = upstream * norm_gain.astype(jnp.float32)
    mean_first = jnp.mean(scaled, axis=-1, keepdims=True)
    mean_second = jnp.mean(scaled * normed, axis=-1, keepdims=True)
    return inverse * (scaled - mean_first - normed * mean_second)


def gelu_parts(preact):
    tanh_part = jnp.tanh(gelu_scale * (preact + gelu_cubic * preact * preact * preact))
    gelu_value = 0.5 * preact * (1.0 + tanh_part)
    gelu_slope = 0.5 * (1.0 + tanh_part) + 0.5 * preact * (
        1.0 - tanh_part * tanh_part
    ) * gelu_scale * (1.0 + 3.0 * gelu_cubic * preact * preact)
    return (gelu_value, gelu_slope)


def masked_scores(queries, keys_half, usable, factor):
    scores = (
        jnp.einsum("bqhd,bkhd->bhqk", queries, keys_half, preferred_element_type=jnp.float32)
        * factor
    )
    return jnp.where(usable[:, None, None, :], scores, masked_score)


def attend(queries, keys_half, values_half, usable, factor):
    scores = masked_scores(queries, keys_half, usable, factor)
    highest = jnp.max(scores, axis=-1, keepdims=True)
    log_total = highest + jnp.log(jnp.sum(jnp.exp(scores - highest), axis=-1, keepdims=True))
    weights = jnp.exp(scores - log_total).astype(jnp.bfloat16)
    mixed_out = jnp.einsum(
        "bhqk,bkhd->bqhd", weights, values_half, preferred_element_type=jnp.float32
    )
    return (mixed_out.astype(jnp.bfloat16), log_total)


def attend_backward(queries, keys_half, values_half, usable, log_total, upstream, factor):
    weights = jnp.exp(masked_scores(queries, keys_half, usable, factor) - log_total)
    value_grad = jnp.einsum(
        "bhqk,bqhd->bkhd",
        weights.astype(jnp.bfloat16),
        upstream,
        preferred_element_type=jnp.float32,
    )
    weight_grad = jnp.einsum(
        "bqhd,bkhd->bhqk", upstream, values_half, preferred_element_type=jnp.float32
    )
    inner_sum = jnp.sum(weights * weight_grad, axis=-1, keepdims=True)
    score_grad = (weights * (weight_grad - inner_sum) * factor).astype(jnp.bfloat16)
    query_grad = jnp.einsum(
        "bhqk,bkhd->bqhd", score_grad, keys_half, preferred_element_type=jnp.float32
    )
    key_grad = jnp.einsum(
        "bhqk,bqhd->bkhd", score_grad, queries, preferred_element_type=jnp.float32
    )
    return (query_grad, key_grad, value_grad)


def row_chunks(rows):
    half = (rows // 2 + 15) // 16 * 16
    if rows < 32 or half >= rows:
        return ((0, rows),)
    return ((0, half), (half, rows - half))


def line_barrier(me, size):
    barrier = pltpu.get_barrier_semaphore()

    @pl.when(me > 0)
    def _():
        pl.semaphore_signal(barrier, inc=1, device_id={"tensor": me - 1}, device_id_type=MESH)

    @pl.when(me < size - 1)
    def _():
        pl.semaphore_signal(barrier, inc=1, device_id={"tensor": me + 1}, device_id_type=MESH)

    inner = jnp.logical_and(me > 0, me < size - 1)

    @pl.when(inner)
    def _():
        pl.semaphore_wait(barrier, 2)

    @pl.when(jnp.logical_not(inner))
    def _():
        pl.semaphore_wait(barrier, 1)


def gather_kernel(size, chunks, x_ref, o_ref, send_r, send_l, recv_r, recv_l):
    me = lax.axis_index("tensor")
    line_barrier(me, size)

    def hop(step, owner, c, rightward):
        start, rows = chunks[c]
        span = pl.ds(start, rows)
        src = x_ref.at[span] if step == 0 else o_ref.at[owner, span]
        send, recv = (send_r, recv_r) if rightward else (send_l, recv_l)
        return pltpu.make_async_remote_copy(
            src_ref=src,
            dst_ref=o_ref.at[owner, span],
            send_sem=send.at[step, c],
            recv_sem=recv.at[owner, c],
            device_id={"tensor": me + 1 if rightward else me - 1},
            device_id_type=MESH,
        )

    for step in range(size):
        for c in range(len(chunks)):
            for rightward in (True, False):
                owner = me - step if rightward else me + step
                valid = owner >= 0 if rightward else owner <= size - 1
                has_next = me < size - 1 if rightward else me > 0

                @pl.when(valid)
                def _():
                    if step > 0:
                        hop(step, owner, c, rightward).wait_recv()
                    if step < size - 1:

                        @pl.when(has_next)
                        def _():
                            hop(step, owner, c, rightward).start()

        if step == 0:
            o_ref[me] = x_ref[...]
    for step in range(size - 1):
        for c in range(len(chunks)):
            for rightward in (True, False):
                owner = me - step if rightward else me + step
                valid = owner >= 0 if rightward else owner <= size - 1
                has_next = me < size - 1 if rightward else me > 0

                @pl.when(jnp.logical_and(valid, has_next))
                def _():
                    hop(step, owner, c, rightward).wait_send()


def scatter_kernel(size, chunks, p_ref, after_ref, o_ref, acc_r, acc_l, send_r, send_l, recv_r, recv_l):
    me = lax.axis_index("tensor")
    line_barrier(me, size)

    def hop(target, c, rightward, first):
        start, rows = chunks[c]
        span = pl.ds(start, rows)
        acc = acc_r if rightward else acc_l
        send, recv = (send_r, recv_r) if rightward else (send_l, recv_l)
        return pltpu.make_async_remote_copy(
            src_ref=p_ref.at[target, span] if first else acc.at[target, span],
            dst_ref=acc.at[target, span],
            send_sem=send.at[target, c],
            recv_sem=recv.at[target, c],
            device_id={"tensor": me + 1 if rightward else me - 1},
            device_id_type=MESH,
        )

    def pass_on(target, c, rightward):
        start, rows = chunks[c]
        span = pl.ds(start, rows)
        acc = acc_r if rightward else acc_l
        is_first = me == 0 if rightward else me == size - 1

        @pl.when(is_first)
        def _():
            hop(target, c, rightward, True).start()

        @pl.when(jnp.logical_not(is_first))
        def _():
            hop(target, c, rightward, False).wait_recv()
            total = acc[target, span].astype(jnp.float32) + p_ref[target, span].astype(jnp.float32)
            acc[target, span] = total.astype(acc.dtype)
            hop(target, c, rightward, False).start()

    for step in range(size - 1):
        for c in range(len(chunks)):
            target_r, target_l = size - 1 - step, step

            @pl.when(me < target_r)
            def _():
                pass_on(target_r, c, True)

            @pl.when(me > target_l)
            def _():
                pass_on(target_l, c, False)

    for c, (start, rows) in enumerate(chunks):
        span = pl.ds(start, rows)
        o_ref[span] = p_ref[me, span].astype(jnp.float32)

        @pl.when(me > 0)
        def _():
            hop(me, c, True, False).wait_recv()
            o_ref[span] += acc_r[me, span].astype(jnp.float32)

        @pl.when(me < size - 1)
        def _():
            hop(me, c, False, False).wait_recv()
            o_ref[span] += acc_l[me, span].astype(jnp.float32)

    for step in range(size - 1):
        for c in range(len(chunks)):
            target_r, target_l = size - 1 - step, step

            @pl.when(me < target_r)
            def _():
                hop(target_r, c, True, False).wait_send()

            @pl.when(me > target_l)
            def _():
                hop(target_l, c, False, False).wait_send()


def exchange_kernel(size, scattered, *refs):
    count = len(scattered)
    ins, outs, (send, recv) = refs[:count], refs[count : 2 * count], refs[2 * count :]
    me = lax.axis_index("dp")
    barrier = pltpu.get_barrier_semaphore()
    for step in range(1, size):
        peer = lax.rem(me + step, size)
        pl.semaphore_signal(barrier, inc=1, device_id={"dp": peer}, device_id_type=MESH)
    pl.semaphore_wait(barrier, size - 1)

    def hop(step, part):
        peer = lax.rem(me + step, size)
        return pltpu.make_async_remote_copy(
            src_ref=ins[part].at[peer] if scattered[part] else ins[part],
            dst_ref=outs[part].at[me],
            send_sem=send.at[step - 1, part],
            recv_sem=recv.at[step - 1, part],
            device_id={"dp": peer},
            device_id_type=MESH,
        )

    for step in range(1, size):
        for part in range(count):
            hop(step, part).start()
    for part in range(count):
        outs[part][me] = ins[part][me] if scattered[part] else ins[part][...]
    for step in range(1, size):
        for part in range(count):
            hop(step, part).wait()


VMEM_SPEC = pl.BlockSpec(memory_space=pltpu.VMEM)


def call_gather(x, size, collective_id):
    rows, width = x.shape
    chunks = row_chunks(rows)
    sems = [
        pltpu.SemaphoreType.DMA((size, len(chunks))) for _ in range(4)
    ]
    return pl.pallas_call(
        functools.partial(gather_kernel, size, chunks),
        out_shape=jax.ShapeDtypeStruct((size, rows, width), x.dtype),
        in_specs=[VMEM_SPEC],
        out_specs=VMEM_SPEC,
        scratch_shapes=sems,
        cost_estimate=pl.CostEstimate(
            flops=rows * width * 100000, bytes_accessed=size * rows * width * 2, transcendentals=0
        ),
        compiler_params=pltpu.CompilerParams(
            collective_id=collective_id, has_side_effects=True, vmem_limit_bytes=16 * 1024 * 1024
        ),
    )(x)


def call_scatter(p, after, collective_id):
    size, rows, width = p.shape
    chunks = row_chunks(rows)
    sems = [
        pltpu.SemaphoreType.DMA((size, len(chunks))) for _ in range(4)
    ]
    return pl.pallas_call(
        functools.partial(scatter_kernel, size, chunks),
        out_shape=jax.ShapeDtypeStruct((rows, width), jnp.float32),
        in_specs=[VMEM_SPEC, pl.BlockSpec(memory_space=pl.ANY)],
        out_specs=VMEM_SPEC,
        scratch_shapes=[pltpu.VMEM(p.shape, p.dtype), pltpu.VMEM(p.shape, p.dtype)] + sems,
        cost_estimate=pl.CostEstimate(
            flops=rows * width * 100000, bytes_accessed=size * rows * width * 2, transcendentals=0
        ),
        compiler_params=pltpu.CompilerParams(
            collective_id=collective_id, has_side_effects=True, vmem_limit_bytes=24 * 1024 * 1024
        ),
    )(p, after)


def call_exchange(parts, scattered, size, collective_id):
    outs = [
        jax.ShapeDtypeStruct(x.shape if flag else (size,) + x.shape, x.dtype)
        for x, flag in zip(parts, scattered)
    ]
    sem = pltpu.SemaphoreType.DMA((size - 1, len(parts)))
    return pl.pallas_call(
        functools.partial(exchange_kernel, size, scattered),
        out_shape=outs,
        in_specs=[VMEM_SPEC] * len(parts),
        out_specs=[VMEM_SPEC] * len(parts),
        scratch_shapes=[sem, sem],
        compiler_params=pltpu.CompilerParams(
            collective_id=collective_id, has_side_effects=True, vmem_limit_bytes=16 * 1024 * 1024
        ),
    )(*parts)


def body(
    block_input,
    key_valid,
    mixgain,
    mixbias,
    inproj_weight,
    querybias,
    valuebias,
    outproj_weight,
    outbias,
    ffgain,
    ffbias,
    expand_weight,
    expbias,
    contract_weight,
    conbias,
    cotangent,
):
    images = block_input.shape[0]
    model_width = block_input.shape[2]
    seq_total = key_valid.shape[1]
    depth_count = inproj_weight.shape[0]
    local_width = inproj_weight.shape[-1]
    local_heads = local_width // HEAD_DIM
    local_hidden = expand_weight.shape[-1]
    shard_width = model_width // lax.axis_size("dp")
    factor = float(HEAD_DIM) ** (-0.5)
    usable = key_valid > 0
    head_shape = (images, seq_total, local_heads, HEAD_DIM)

    tensor_size = lax.axis_size("tensor")
    data_size = lax.axis_size("dp")
    vectors = jnp.stack(
        [mixgain, mixbias, outbias, ffgain, ffbias, conbias]
    )
    shared = jnp.pad(
        vectors.reshape(6 * depth_count, shard_width), ((0, -6 * depth_count % 16), (0, 0))
    )
    (vectors_full,) = call_exchange([shared], (False,), data_size, 3)
    vectors_full = (
        jnp.swapaxes(vectors_full[:, : 6 * depth_count], 0, 1)
        .reshape(6, depth_count, model_width)
    )

    big_gather = jax.jit(lambda x: call_gather(x, tensor_size, 0))
    big_scatter = jax.jit(lambda p, after: call_scatter(p, after, 1))

    def gather_rows(x):
        local = x.shape[1]
        full = big_gather(x.reshape(images * local, model_width))
        full = full.reshape(tensor_size, images, local, model_width)
        return jnp.swapaxes(full, 0, 1).reshape(images, seq_total, model_width)

    def scatter_weight(grad, dimension):
        return lax.psum_scatter(grad, "dp", scatter_dimension=dimension, tiled=True)

    def scatter_rows(p, *earlier):
        pieces = [x[:1, :128].astype(p.dtype) for x in earlier]
        pieces += [jnp.zeros((1, 128), p.dtype)] * (8 - len(pieces))
        after = jnp.concatenate(pieces)
        local = seq_total // tensor_size
        split = jnp.swapaxes(p.reshape(images, tensor_size, local, model_width), 0, 1)
        part = big_scatter(split.reshape(tensor_size, images * local, model_width), after)
        return part.reshape(images, local, model_width)

    def fetch_attention(layer_index):
        shard = jnp.concatenate([inproj_weight[layer_index], outproj_weight[layer_index].T[None]])
        full = lax.all_gather(shard, "dp", axis=1, tiled=True)
        return (full[:3], full[3]) + tuple(vectors_full[:3, layer_index])

    def fetch_dense(layer_index):
        shard = jnp.stack([expand_weight[layer_index], contract_weight[layer_index].T])
        full = lax.all_gather(shard, "dp", axis=1, tiled=True)
        return (full[0], full[1]) + tuple(vectors_full[3:, layer_index])

    residual = block_input
    stored = []
    for layer_index in range(depth_count):
        attention_pack = fetch_attention(layer_index)
        inproj_full, outproj_full, mix_gain, mix_shift, out_shift = attention_pack
        mix_value, mix_normed, mix_inverse = layer_norm(residual, mix_gain, mix_shift)
        mix_rows = gather_rows(mix_value.astype(jnp.bfloat16))
        projected = jnp.einsum(
            "bsd,cde->cbse", mix_rows, inproj_full, preferred_element_type=jnp.float32
        )
        queries = (
            (projected[0] + querybias[layer_index].astype(jnp.float32))
            .astype(jnp.bfloat16)
            .reshape(head_shape)
        )
        keys_half = projected[1].astype(jnp.bfloat16).reshape(head_shape)
        values_half = (
            (projected[2] + valuebias[layer_index].astype(jnp.float32))
            .astype(jnp.bfloat16)
            .reshape(head_shape)
        )
        heads_out, log_total = attend(queries, keys_half, values_half, usable, factor)
        heads_flat = heads_out.reshape(images, seq_total, local_width)
        partial_out = jnp.einsum(
            "bse,de->bsd", heads_flat, outproj_full, preferred_element_type=jnp.float32
        )
        middle = (
            residual
            + scatter_rows(partial_out.astype(jnp.bfloat16))
            + out_shift.astype(jnp.float32)
        )
        dense_pack = fetch_dense(layer_index)
        expand_full, contract_full, ff_gain, ff_shift, con_shift = dense_pack
        ff_value, ff_normed, ff_inverse = layer_norm(middle, ff_gain, ff_shift)
        ff_rows = gather_rows(ff_value.astype(jnp.bfloat16))
        preact = jnp.einsum(
            "bsd,df->bsf", ff_rows, expand_full, preferred_element_type=jnp.float32
        ) + expbias[layer_index].astype(jnp.float32)
        gelu_value, gelu_slope = gelu_parts(preact)
        hidden_half = gelu_value.astype(jnp.bfloat16)
        partial_dense = jnp.einsum(
            "bsf,df->bsd", hidden_half, contract_full, preferred_element_type=jnp.float32
        )
        stored.append(
            (
                mix_normed,
                mix_inverse,
                mix_rows,
                queries,
                keys_half,
                values_half,
                log_total,
                heads_flat,
                ff_normed,
                ff_inverse,
                ff_rows,
                gelu_slope,
                hidden_half,
                attention_pack,
                dense_pack,
            )
        )
        residual = (
            middle
            + scatter_rows(partial_dense.astype(jnp.bfloat16))
            + con_shift.astype(jnp.float32)
        )
    upstream = cotangent
    layer_results = [None] * depth_count
    for layer_index in reversed(range(depth_count)):
        (
            mix_normed,
            mix_inverse,
            mix_rows,
            queries,
            keys_half,
            values_half,
            log_total,
            heads_flat,
            ff_normed,
            ff_inverse,
            ff_rows,
            gelu_slope,
            hidden_half,
            attention_pack,
            dense_pack,
        ) = stored[layer_index]
        expand_full, contract_full, ff_gain, ff_shift, con_shift = dense_pack
        upstream_half = upstream.astype(jnp.bfloat16)
        upstream_rows = gather_rows(upstream_half)
        contract_grad = jnp.einsum(
            "bsd,bsf->df", upstream_rows, hidden_half, preferred_element_type=jnp.float32
        )
        preact_grad = (
            jnp.einsum(
                "bsd,df->bsf", upstream_rows, contract_full, preferred_element_type=jnp.float32
            )
            * gelu_slope
        )
        preact_half = preact_grad.astype(jnp.bfloat16)
        expand_grad = jnp.einsum(
            "bsd,bsf->df", ff_rows, preact_half, preferred_element_type=jnp.float32
        )
        ff_partial = jnp.einsum(
            "bsf,df->bsd", preact_half, expand_full, preferred_element_type=jnp.float32
        )
        ff_partial, contract_half, expand_half = lax.optimization_barrier(
            (
                ff_partial.astype(jnp.bfloat16),
                contract_grad.astype(jnp.bfloat16),
                expand_grad.astype(jnp.bfloat16),
            )
        )
        dense_half = jnp.concatenate([expand_half, contract_half], axis=1)
        dense_part = scatter_weight(dense_half, 0)
        ff_back = scatter_rows(ff_partial, dense_half)
        middle_grad = upstream + norm_backward(ff_back, ff_normed, ff_inverse, ff_gain)
        inproj_full, outproj_full, mix_gain, mix_shift, out_shift = attention_pack
        middle_rows = gather_rows(middle_grad.astype(jnp.bfloat16))
        outproj_grad = jnp.einsum(
            "bsd,bse->de", middle_rows, heads_flat, preferred_element_type=jnp.float32
        )
        middle_rows, outproj_half = lax.optimization_barrier(
            (middle_rows, outproj_grad.astype(jnp.bfloat16))
        )
        heads_grad = (
            jnp.einsum("bsd,de->bse", middle_rows, outproj_full, preferred_element_type=jnp.float32)
            .astype(jnp.bfloat16)
            .reshape(head_shape)
        )
        query_grad, key_grad, value_grad = attend_backward(
            queries, keys_half, values_half, usable, log_total, heads_grad, factor
        )
        proj_grad = jnp.stack([query_grad, key_grad, value_grad]).reshape(
            3, images, seq_total, local_width
        )
        proj_half = proj_grad.astype(jnp.bfloat16)
        inproj_grad = jnp.einsum(
            "bsd,cbse->dce", mix_rows, proj_half, preferred_element_type=jnp.float32
        )
        mix_partial = jnp.einsum(
            "cbse,cde->bsd", proj_half, inproj_full, preferred_element_type=jnp.float32
        )
        mix_partial, inproj_half = lax.optimization_barrier(
            (mix_partial.astype(jnp.bfloat16), inproj_grad.astype(jnp.bfloat16))
        )
        attention_half = jnp.concatenate(
            [inproj_half.reshape(model_width, 3 * local_width), outproj_half], axis=1
        )
        attention_part = scatter_weight(attention_half, 0)
        mix_back = scatter_rows(mix_partial, attention_half)
        upstream_next = middle_grad + norm_backward(mix_back, mix_normed, mix_inverse, mix_gain)
        query_sum = jnp.sum(proj_grad[0], axis=(0, 1))
        value_sum = jnp.sum(proj_grad[2], axis=(0, 1))
        expand_sum = jnp.sum(preact_grad, axis=(0, 1))
        side = max(local_width, local_hidden)
        tensor_rows = jnp.stack(
            [
                jnp.pad(query_sum, (0, side - local_width)),
                jnp.pad(value_sum, (0, side - local_width)),
                jnp.pad(expand_sum, (0, side - local_hidden)),
            ]
        )
        vector_rows = jnp.stack(
            [
                jnp.sum(mix_back * mix_normed, axis=(0, 1)),
                jnp.sum(mix_back, axis=(0, 1)),
                jnp.sum(middle_grad, axis=(0, 1)),
                jnp.sum(ff_back * ff_normed, axis=(0, 1)),
                jnp.sum(ff_back, axis=(0, 1)),
                jnp.sum(upstream, axis=(0, 1)),
            ]
        )
        weight_parts = tuple(
            part.astype(jnp.float32)
            for part in (
                jnp.swapaxes(
                    attention_part[:, : 3 * local_width].reshape(shard_width, 3, local_width), 0, 1
                ),
                attention_part[:, 3 * local_width :].T,
                dense_part[:, :local_hidden],
                dense_part[:, local_hidden:].T,
            )
        )
        layer_results[layer_index] = (weight_parts, vector_rows, tensor_rows)
        upstream = upstream_next
    inproj_list = []
    outproj_list = []
    expand_list = []
    contract_list = []
    vector_list = []
    expbias_list = []
    for position in range(depth_count):
        weight_parts, vector_rows, tensor_rows = layer_results[position]
        inproj_list.append(weight_parts[0])
        outproj_list.append(weight_parts[1])
        expand_list.append(weight_parts[2])
        contract_list.append(weight_parts[3])
        vector_list.append(vector_rows)
        expbias_list.append(tensor_rows)
    inproj_out, outproj_out, expand_out, contract_out = (
        jnp.stack(inproj_list),
        jnp.stack(outproj_list),
        jnp.stack(expand_list),
        jnp.stack(contract_list),
    )
    kinds = 6
    data_rows = jnp.swapaxes(
        jnp.stack(vector_list).reshape(depth_count * kinds, data_size, shard_width), 0, 1
    )
    tensor_rows = jnp.stack(expbias_list).reshape(depth_count * 3, -1)
    data_all, tensor_all = call_exchange([data_rows, tensor_rows], (True, False), data_size, 2)
    tensor_part = jnp.sum(tensor_all, axis=0).reshape(depth_count, 3, -1)
    data_line = call_gather(jnp.sum(data_all, axis=0), tensor_size, 4)
    data_part = jnp.sum(data_line, axis=0).reshape(depth_count, kinds, shard_width)
    query_part = tensor_part[:, 0, :local_width]
    value_part = tensor_part[:, 1, :local_width]
    expbias_part = tensor_part[:, 2, :local_hidden]
    return (
        residual,
        upstream,
        data_part[:, 0],
        data_part[:, 1],
        inproj_out,
        query_part,
        value_part,
        outproj_out,
        data_part[:, 2],
        data_part[:, 3],
        data_part[:, 4],
        expand_out,
        expbias_part,
        contract_out,
        data_part[:, 5],
    )


def solution(mesh):
    return jax.shard_map(
        body,
        mesh=mesh,
        in_specs=(
            P("dp", "tensor", None),
            P("dp", None),
            P(None, "dp"),
            P(None, "dp"),
            P(None, None, "dp", "tensor"),
            P(None, "tensor"),
            P(None, "tensor"),
            P(None, "tensor", "dp"),
            P(None, "dp"),
            P(None, "dp"),
            P(None, "dp"),
            P(None, "dp", "tensor"),
            P(None, "tensor"),
            P(None, "tensor", "dp"),
            P(None, "dp"),
            P("dp", "tensor", None),
        ),
        out_specs=(
            P("dp", "tensor", None),
            P("dp", "tensor", None),
            P(None, "dp"),
            P(None, "dp"),
            P(None, None, "dp", "tensor"),
            P(None, "tensor"),
            P(None, "tensor"),
            P(None, "tensor", "dp"),
            P(None, "dp"),
            P(None, "dp"),
            P(None, "dp"),
            P(None, "dp", "tensor"),
            P(None, "tensor"),
            P(None, "tensor", "dp"),
            P(None, "dp"),
        ),
        check_vma=False,
    )
```
